32 devices in a mesh: ctx: 8 (over z, y), head: 4 (over x, core).
Axes of the slice: x: 2, y: 2, z: 4, core: 2. Of those that a mesh axis runs over, the one named last changes fastest.
Arguments:
- x_in: bfloat16 [4096, 1024], P(('ctx', 'head')), may hold values from -6 to 6
- in_weight: bfloat16 [1024, 4120], P(('ctx', 'head')), may hold values from -1 to 1
- out_weight: bfloat16 [2048, 1024], P(('ctx', 'head')), may hold values from -0.1875 to 0.1875
- gu_weight: bfloat16 [1024, 4096], P(('ctx', 'head')), may hold values from -0.1875 to 0.1875
- down_weight: bfloat16 [2048, 1024], P(('ctx', 'head')), may hold values from -0.125 to 0.125
- norm_gain: bfloat16 [1024], P(('ctx', 'head')), may hold values from 0.5 to 1.5
- mixer_gain: bfloat16 [1536], P(('ctx', 'head')), may hold values from 0.5 to 1.5
- ffn_gain: bfloat16 [1024], P(('ctx', 'head')), may hold values from 0.5 to 1.5
- conv_weight: bfloat16 [1792, 4], P(('ctx', 'head')), may hold values from -3 to 3
- conv_bias: bfloat16 [1792], P(('ctx', 'head')), may hold values from -3 to 3
- dt_bias: float32 [24], P('head'), may hold values from -1 to 1
- a_log: float32 [24], P('head'), may hold values from -14 to -2
- skip_gain: float32 [24], P('head'), may hold values from 0 to 2
- out_grad: bfloat16 [4096, 1024], P(('ctx', 'head')), may hold values from -6 to 6
Outputs:
- y_out: bfloat16 [4096, 1024], P(('ctx', 'head'))
- x_grad: float32 [4096, 1024], P(('ctx', 'head'))
- in_weight_grad: float32 [1024, 4120], P(('ctx', 'head'))
- out_weight_grad: float32 [2048, 1024], P(('ctx', 'head'))
- gu_weight_grad: float32 [1024, 4096], P(('ctx', 'head'))
- down_weight_grad: float32 [2048, 1024], P(('ctx', 'head'))
- norm_gain_grad: float32 [1024], P(('ctx', 'head'))
- mixer_gain_grad: float32 [1536], P(('ctx', 'head'))
- ffn_gain_grad: float32 [1024], P(('ctx', 'head'))
- conv_weight_grad: float32 [1792, 4], P(('ctx', 'head'))
- conv_bias_grad: float32 [1792], P(('ctx', 'head'))
- dt_bias_grad: float32 [24], P('head')
- a_log_grad: float32 [24], P('head')
- skip_grad: float32 [24], P('head')
The draws below stay inside these ranges and needn't reach their ends.
All inputs are finite; a program needn't handle non-finite values.
Results may differ from the reference program's by a relative error of at most 0.018.
The reference program's roundings to bfloat16 on the way count: a program that leaves them out, or rounds other values in their place, can miss the bound.
Values may be sent and summed in bfloat16 or wider, within the bound.
A program may use at most 192 MiB of HBM per device.

```python
import math
import jax
import jax.numpy as jnp
from jax import lax

D = 1024
FF = 2048
MH = 24
MP = 64
NS = 128
KW = 4
AH = 8
KVH = 2
HDIM = 64
SB = 256
TOK_DEV = 128
L = 4096
DSSM = 1536
CONVCH = 1792
NPROJ = 4120
NOUT = 2048
N_HEAD = 4


def shared_pattern(key):
    base = jax.random.fold_in(key, 9001)
    rate_dir = jnp.where(jax.random.bernoulli(jax.random.fold_in(base, 3), 0.5, (D,)), 1.0, -1.0).astype(jnp.float32)
    return rate_dir


def range_offsets(key):
    range_rows = TOK_DEV * N_HEAD
    ranges = L // range_rows
    base = jax.random.fold_in(key, 7001)
    order = jax.random.permutation(jax.random.fold_in(base, 1), ranges).astype(jnp.float32)
    jitter = jax.random.uniform(jax.random.fold_in(base, 2), (ranges,), jnp.float32)
    levels = -1.0 + 2.0 * (order + jitter) / ranges
    return jnp.repeat(levels, range_rows)


def draw_x_in(key, part):
    rate_dir = shared_pattern(key)
    offsets = range_offsets(key)[:, None] * rate_dir[None, :]
    values = jax.random.normal(jax.random.fold_in(key, 1), (L, D), jnp.float32) + offsets
    return jnp.clip(values, -6.0, 6.0).astype(jnp.bfloat16)


def draw_in_weight(key, part):
    values = jnp.clip(jax.random.normal(jax.random.fold_in(key, 2), (D, NPROJ), jnp.float32), -6.0, 6.0) / math.sqrt(D)
    rate_dir = shared_pattern(key)
    rate_start = 2 * MH * MP + 2 * NS
    rate_extra = 4.0 * rate_dir[:, None] * jnp.ones((1, MH), jnp.float32) / D
    values = jnp.concatenate([values[:, :rate_start], values[:, rate_start:rate_start + MH] + rate_extra, values[:, rate_start + MH:]], axis=1)
    return jnp.clip(values, -1.0, 1.0).astype(jnp.bfloat16)


def steps_of(rng, shape, cuts, smallest, largest):
    factor_of = 1.0
    for dim, shards_of in cuts:
        draws = jax.random.uniform(jax.random.fold_in(jax.random.fold_in(rng, 6), dim), (shards_of,), jnp.float32, smallest / len(cuts), largest / len(cuts))
        factor_of = factor_of * jnp.repeat(jnp.exp(draws), shape[dim] // shards_of).reshape((-1,) + (1,) * (len(shape) - 1 - dim))
    return factor_of


def noise(stream_key, shape, width, most, split=(), dtype=jnp.bfloat16):
    values = width * jax.random.normal(stream_key, shape, jnp.float32)
    if split:
        values = values * steps_of(stream_key, shape, split, -0.22, 0.18)
    return jnp.clip(values, -most, most).astype(dtype)


def setup_inputs(seed: int = 0) -> dict:
    seeds = jax.random.split(jax.random.key(seed), 15)
    return {
        "x_in": draw_x_in(jax.random.fold_in(seeds[14], 71), 0),
        "in_weight": draw_in_weight(jax.random.fold_in(seeds[14], 71), 0),
        "out_weight": noise(seeds[2], (NOUT, D), (NOUT // 2) ** -0.5, 0.1875, ((0, 32),)),
        "gu_weight": noise(seeds[3], (D, 2 * FF), D ** -0.5, 0.1875, ((0, 32),)),
        "down_weight": noise(seeds[4], (FF, D), FF ** -0.5, 0.125, ((0, 32),)),
        "norm_gain": jnp.clip(1.0 + 0.1 * jax.random.normal(seeds[5], (D,), jnp.float32), 0.5, 1.5).astype(jnp.bfloat16),
        "mixer_gain": jnp.clip(1.0 + 0.1 * jax.random.normal(seeds[6], (DSSM,), jnp.float32), 0.5, 1.5).astype(jnp.bfloat16),
        "ffn_gain": jnp.clip(1.0 + 0.1 * jax.random.normal(seeds[7], (D,), jnp.float32), 0.5, 1.5).astype(jnp.bfloat16),
        "conv_weight": noise(seeds[8], (CONVCH, KW), KW ** -0.5, 3.0, ((0, 32),)),
        "conv_bias": noise(seeds[9], (CONVCH,), 0.5, 3.0, ((0, 32),)),
        "dt_bias": jnp.clip(jax.random.uniform(seeds[10], (MH,), jnp.float32, -1.0, 1.0) * steps_of(seeds[10], (MH,), ((0, 4),), -0.4, 0.0), -1.0, 1.0),
        "a_log": jnp.clip(-14.0 + 12.0 * jax.random.uniform(seeds[11], (MH,), jnp.float32) ** steps_of(seeds[11], (MH,), ((0, 4),), -0.2, 0.2), -14.0, -2.0),
        "skip_gain": jnp.clip(2.0 * jax.random.uniform(seeds[12], (MH,), jnp.float32) ** steps_of(seeds[12], (MH,), ((0, 4),), -0.2, 0.2), 0.0, 2.0),
        "out_grad": noise(seeds[13], (L, D), 1.0, 6.0, ((0, 32),)),
    }


EPSILON = 1e-05
ROPE_BASE = 10000.0
PRECISE_MODE = lax.Precision.HIGHEST

def silu_grad(value):
    sigmoid = jax.nn.sigmoid(value)
    return sigmoid * (1.0 + value * (1.0 - sigmoid))

def rotate_pairs(values, positions, direction):
    half_dim = values.shape[-1] // 2
    inverse = ROPE_BASE ** (-jnp.arange(half_dim).astype(jnp.float32) / half_dim)
    angles = positions[:, None] * inverse[None, :]
    cosine = jnp.cos(angles)[:, None, :]
    sine = direction * jnp.sin(angles)[:, None, :]
    first_half = values[..., :half_dim]
    second_half = values[..., half_dim:]
    return jnp.concatenate([first_half * cosine - second_half * sine, second_half * cosine + first_half * sine], axis=-1)

def state_block(state, pieces, decay_rate, skip_gain):
    inputs_x, bmat, cmat, step_size = pieces
    length = inputs_x.shape[0]
    cumulative = jnp.cumsum(step_size * decay_rate[None, :], axis=0)
    lower = (jnp.arange(length)[:, None] >= jnp.arange(length)[None, :])[None, :, :]
    spread = cumulative.T[:, :, None] - cumulative.T[:, None, :]
    within = jnp.where(lower, jnp.exp(jnp.where(lower, spread, 0.0)), 0.0)
    scaled_x = inputs_x * step_size[:, :, None]
    products = jnp.dot(cmat, bmat.T, precision=PRECISE_MODE)
    intra = jnp.einsum('ts,hts,shp->thp', products, within, scaled_x, precision=PRECISE_MODE)
    inter = jnp.einsum('tn,hpn->thp', cmat, state, precision=PRECISE_MODE) * jnp.exp(cumulative)[:, :, None]
    remain = jnp.exp(cumulative[-1][None, :] - cumulative)
    new_state = jnp.exp(cumulative[-1])[:, None, None] * state + jnp.einsum('sh,shp,sn->hpn', remain, scaled_x, bmat, precision=PRECISE_MODE)
    return (new_state, intra + inter + skip_gain[None, :, None] * inputs_x)

def mixer_local(inputs_x, bmat, cmat, step_size, decay_rate, skip_gain, state):
    count = inputs_x.shape[0] // SB

    def advance(carry, pieces):
        return state_block(carry, pieces, decay_rate, skip_gain)

    def shaped(value):
        return value.reshape((count, SB) + value.shape[1:])
    final, outputs = lax.scan(advance, state, (shaped(inputs_x), shaped(bmat), shaped(cmat), shaped(step_size)))
    return (outputs.reshape(inputs_x.shape), final)

def reference(x_in, in_weight, out_weight, gu_weight, down_weight, norm_gain, mixer_gain, ffn_gain, conv_weight, conv_bias, dt_bias, a_log, skip_gain, out_grad):
    float_type = jnp.float32
    half_type = jnp.bfloat16
    total = x_in.shape[0]
    dssm_cols = MH * MP
    conv_cols = dssm_cols + 2 * NS
    query_start = 2 * dssm_cols + 2 * NS + MH
    key_start = query_start + AH * HDIM
    value_start = key_start + KVH * HDIM
    group_size = AH // KVH
    score_scale = 1.0 / math.sqrt(HDIM)
    block_rows = 512
    block_count = total // block_rows
    inputs = x_in.astype(float_type)
    gain_one = norm_gain.astype(float_type)
    gain_mix = mixer_gain.astype(float_type)
    gain_two = ffn_gain.astype(float_type)
    conv_w = conv_weight.astype(float_type)
    conv_b = conv_bias.astype(float_type)
    rms_in = lax.rsqrt(lax.optimization_barrier(jnp.mean(inputs * inputs, axis=1, keepdims=True)) + EPSILON)
    normed = (inputs * rms_in * gain_one[None, :]).astype(half_type)
    proj = jnp.dot(normed, in_weight, preferred_element_type=float_type).astype(half_type)
    z_part = proj[:, :dssm_cols].astype(float_type)
    padded = jnp.concatenate([jnp.zeros((KW - 1, conv_cols), float_type), proj[:, dssm_cols:dssm_cols + conv_cols].astype(float_type)], axis=0)
    conv_pre = jnp.broadcast_to(conv_b[None, :], (total, conv_cols))
    for offset in range(KW):
        conv_pre = conv_pre + padded[offset:offset + total] * conv_w[:, offset][None, :]
    conv_out = jax.nn.silu(conv_pre).astype(half_type)
    mix_x = conv_out[:, :dssm_cols].astype(float_type).reshape(total, MH, MP)
    bmat = conv_out[:, dssm_cols:dssm_cols + NS].astype(float_type)
    cmat = conv_out[:, dssm_cols + NS:].astype(float_type)
    dt_pre = proj[:, dssm_cols + conv_cols:query_start].astype(float_type) + dt_bias[None, :]
    step_size = jax.nn.softplus(dt_pre)
    decay_rate = -jnp.exp(a_log)

    def mixer_map(mix_in, b_in, c_in, step_in, decay_in, skip_in):
        return mixer_local(mix_in, b_in, c_in, step_in, decay_in, skip_in, jnp.zeros((MH, MP, NS), float_type))[0]
    ssm_full, ssm_pull = jax.vjp(mixer_map, mix_x, bmat, cmat, step_size, decay_rate, skip_gain)
    ssm_out = ssm_full.reshape(total, dssm_cols).astype(half_type)
    positions = jnp.arange(total).astype(float_type)
    q_rot = rotate_pairs(proj[:, query_start:key_start].astype(float_type).reshape(total, AH, HDIM), positions, 1.0).astype(half_type)
    k_rot = rotate_pairs(proj[:, key_start:value_start].astype(float_type).reshape(total, KVH, HDIM), positions, 1.0).astype(half_type)
    keys_all = jnp.repeat(k_rot, group_size, axis=1).astype(float_type)
    values_all = jnp.repeat(proj[:, value_start:].reshape(total, KVH, HDIM), group_size, axis=1).astype(float_type)
    queries_all = q_rot.astype(float_type)

    def block_scores(query_blk, key_blk, query_first, key_first):
        raw = jnp.einsum('thd,uhd->thu', query_blk, key_blk) * score_scale
        valid = (key_first + jnp.arange(block_rows))[None, None, :] <= (query_first + jnp.arange(block_rows))[:, None, None]
        return jnp.where(valid, raw, -jnp.inf)

    def attend(number):
        query_first = number * block_rows
        query_blk = lax.dynamic_slice_in_dim(queries_all, query_first, block_rows, 0)

        def stat_step(other, carry):
            row_peak, row_mass = carry
            scores = block_scores(query_blk, lax.dynamic_slice_in_dim(keys_all, other * block_rows, block_rows, 0), query_first, other * block_rows)
            new_peak = jnp.maximum(row_peak, lax.optimization_barrier(jnp.max(scores, axis=2)))
            row_mass = row_mass * jnp.exp(row_peak - new_peak) + lax.optimization_barrier(jnp.sum(jnp.exp(scores - new_peak[:, :, None]), axis=2))
            return (new_peak, row_mass)
        row_peak, row_mass = lax.fori_loop(0, number + 1, stat_step, (jnp.full((block_rows, AH), -jnp.inf, float_type), jnp.zeros((block_rows, AH), float_type)))
        log_total = row_peak + jnp.log(row_mass)

        def out_step(other, accum):
            scores = block_scores(query_blk, lax.dynamic_slice_in_dim(keys_all, other * block_rows, block_rows, 0), query_first, other * block_rows)
            probs = lax.optimization_barrier(jnp.exp(scores - log_total[:, :, None]).astype(half_type)).astype(float_type)
            return accum + jnp.einsum('thu,uhd->thd', probs, lax.dynamic_slice_in_dim(values_all, other * block_rows, block_rows, 0))
        attn_blk = lax.fori_loop(0, number + 1, out_step, jnp.zeros((block_rows, AH, HDIM), float_type))
        return (attn_blk.astype(half_type), log_total)
    attn_blocks, log_blocks = lax.map(attend, jnp.arange(block_count))
    attn = attn_blocks.reshape(total, AH * HDIM)
    log_all = log_blocks.reshape(total, AH)
    gated = ssm_out.astype(float_type) * jax.nn.silu(z_part)
    rms_mix = lax.rsqrt(lax.optimization_barrier(jnp.mean(gated * gated, axis=1, keepdims=True)) + EPSILON)
    mixed_norm = (gated * rms_mix * gain_mix[None, :]).astype(half_type)
    joined = jnp.concatenate([mixed_norm, attn], axis=1)
    residual = inputs + jnp.dot(joined, out_weight, preferred_element_type=float_type)
    rms_ffn = lax.rsqrt(lax.optimization_barrier(jnp.mean(residual * residual, axis=1, keepdims=True)) + EPSILON)
    normed_ffn = (residual * rms_ffn * gain_two[None, :]).astype(half_type)
    gate_up = jnp.dot(normed_ffn, gu_weight, preferred_element_type=float_type)
    gate_part = gate_up[:, :FF]
    up_part = gate_up[:, FF:]
    activ = (jax.nn.silu(gate_part) * up_part).astype(half_type)
    y_out = (residual + jnp.dot(activ, down_weight, preferred_element_type=float_type)).astype(half_type)
    d_activ = jnp.dot(out_grad, down_weight.T, preferred_element_type=float_type)
    down_grad = jnp.dot(activ.T, out_grad, preferred_element_type=float_type)
    d_gate_up = jnp.concatenate([d_activ * up_part * silu_grad(gate_part), d_activ * jax.nn.silu(gate_part)], axis=1).astype(half_type)
    d_normed_ffn = jnp.dot(d_gate_up, gu_weight.T, preferred_element_type=float_type)
    gu_grad = jnp.dot(normed_ffn.T, d_gate_up, preferred_element_type=float_type)
    ffn_gain_grad = lax.optimization_barrier(jnp.sum(d_normed_ffn * residual * rms_ffn, axis=0))
    scaled_ffn = gain_two[None, :] * d_normed_ffn
    d_residual = out_grad.astype(float_type) + rms_ffn * scaled_ffn - residual * rms_ffn ** 3 * lax.optimization_barrier(jnp.mean(scaled_ffn * residual, axis=1, keepdims=True))
    d_res_half = d_residual.astype(half_type)
    d_joined = jnp.dot(d_res_half, out_weight.T, preferred_element_type=float_type)
    out_weight_grad = jnp.dot(joined.T, d_res_half, preferred_element_type=float_type)
    d_mixed = d_joined[:, :dssm_cols]
    d_attn = d_joined[:, dssm_cols:].astype(half_type)
    mixer_gain_grad = lax.optimization_barrier(jnp.sum(d_mixed * gated * rms_mix, axis=0))
    scaled_mix = gain_mix[None, :] * d_mixed
    d_gated = rms_mix * scaled_mix - gated * rms_mix ** 3 * lax.optimization_barrier(jnp.mean(scaled_mix * gated, axis=1, keepdims=True))
    d_ssm = (d_gated * jax.nn.silu(z_part)).astype(half_type)
    d_z = d_gated * ssm_out.astype(float_type) * silu_grad(z_part)
    d_attn_all = d_attn.astype(float_type).reshape(total, AH, HDIM)
    row_delta = lax.optimization_barrier(jnp.sum(d_attn_all * attn.astype(float_type).reshape(total, AH, HDIM), axis=2))

    def back_block(carry, number):
        key_grads, value_grads = carry
        query_first = number * block_rows
        query_blk = lax.dynamic_slice_in_dim(queries_all, query_first, block_rows, 0)
        grad_blk = lax.dynamic_slice_in_dim(d_attn_all, query_first, block_rows, 0)
        log_blk = lax.dynamic_slice_in_dim(log_all, query_first, block_rows, 0)
        delta_blk = lax.dynamic_slice_in_dim(row_delta, query_first, block_rows, 0)

        def inner(other, state):
            query_grad, key_acc, value_acc = state
            key_first = other * block_rows
            key_blk = lax.dynamic_slice_in_dim(keys_all, key_first, block_rows, 0)
            value_blk = lax.dynamic_slice_in_dim(values_all, key_first, block_rows, 0)
            probs = jnp.exp(block_scores(query_blk, key_blk, query_first, key_first) - log_blk[:, :, None])
            probs_half = lax.optimization_barrier(probs.astype(half_type)).astype(float_type)
            d_probs = jnp.einsum('thd,uhd->thu', grad_blk, value_blk)
            d_scores = lax.optimization_barrier((probs * (d_probs - delta_blk[:, :, None])).astype(half_type)).astype(float_type)
            query_grad = query_grad + jnp.einsum('thu,uhd->thd', d_scores, key_blk) * score_scale
            key_part = jnp.einsum('thu,thd->uhd', d_scores, query_blk) * score_scale
            value_part = jnp.einsum('thu,thd->uhd', probs_half, grad_blk)
            key_acc = lax.dynamic_update_slice_in_dim(key_acc, lax.dynamic_slice_in_dim(key_acc, key_first, block_rows, 0) + key_part, key_first, 0)
            value_acc = lax.dynamic_update_slice_in_dim(value_acc, lax.dynamic_slice_in_dim(value_acc, key_first, block_rows, 0) + value_part, key_first, 0)
            return (query_grad, key_acc, value_acc)
        query_grad, key_grads, value_grads = lax.fori_loop(0, number + 1, inner, (jnp.zeros((block_rows, AH, HDIM), float_type), key_grads, value_grads))
        return ((key_grads, value_grads), query_grad)
    zero_keys = jnp.zeros((total, AH, HDIM), float_type)
    (key_grads, value_grads), query_grads = lax.scan(back_block, (zero_keys, zero_keys), jnp.arange(block_count))
    d_query = rotate_pairs(query_grads.reshape(total, AH, HDIM), positions, -1.0).reshape(total, AH * HDIM)
    d_key = rotate_pairs(lax.optimization_barrier(jnp.sum(key_grads.reshape(total, KVH, group_size, HDIM), axis=2)), positions, -1.0).reshape(total, KVH * HDIM)
    d_value = lax.optimization_barrier(jnp.sum(value_grads.reshape(total, KVH, group_size, HDIM), axis=2)).reshape(total, KVH * HDIM)
    grad_x, grad_b, grad_c, grad_step, grad_decay, skip_grad = ssm_pull(d_ssm.astype(float_type).reshape(total, MH, MP))
    d_dt_pre = grad_step * jax.nn.sigmoid(dt_pre)
    dt_bias_grad = lax.optimization_barrier(jnp.sum(d_dt_pre, axis=0))
    a_log_grad = grad_decay * decay_rate
    d_conv_pre = jnp.concatenate([grad_x.reshape(total, dssm_cols), grad_b, grad_c], axis=1) * silu_grad(conv_pre)
    conv_bias_grad = lax.optimization_barrier(jnp.sum(d_conv_pre, axis=0))
    conv_weight_grad = jnp.stack([lax.optimization_barrier(jnp.sum(d_conv_pre * padded[offset:offset + total], axis=0)) for offset in range(KW)], axis=1)
    d_padded = jnp.zeros((total + KW - 1, conv_cols), float_type)
    for offset in range(KW):
        d_padded = d_padded + jnp.pad(d_conv_pre * conv_w[:, offset][None, :], ((offset, KW - 1 - offset), (0, 0)))
    d_xbc = d_padded[KW - 1:]
    d_proj = jnp.concatenate([d_z, d_xbc, d_dt_pre, d_query, d_key, d_value], axis=1).astype(half_type)
    d_normed = jnp.dot(d_proj, in_weight.T, preferred_element_type=float_type)
    in_grad = jnp.dot(normed.T, d_proj, preferred_element_type=float_type)
    norm_gain_grad = lax.optimization_barrier(jnp.sum(d_normed * inputs * rms_in, axis=0))
    scaled_in = gain_one[None, :] * d_normed
    x_grad = d_residual + rms_in * scaled_in - inputs * rms_in ** 3 * lax.optimization_barrier(jnp.mean(scaled_in * inputs, axis=1, keepdims=True))
    return (y_out, x_grad, in_grad, out_weight_grad, gu_grad, down_grad, norm_gain_grad, mixer_gain_grad, ffn_gain_grad, conv_weight_grad, conv_bias_grad, dt_bias_grad, a_log_grad, skip_grad)
```

```python
import math

import jax
import jax.numpy as jnp
from jax import lax
from jax.sharding import PartitionSpec as P

FF = 2048
MH = 24
MP = 64
NS = 128
KW = 4
AH = 8
KVH = 2
HDIM = 64
CHUNK = 128


EPSILON = 1e-05
ROPE_BASE = 10000.0
PRECISE_MODE = lax.Precision.HIGHEST


def passed_along(block, axis, distance):
    devices = range(lax.axis_size(axis))
    route = [(i - distance, i) for i in devices if i - distance in devices]
    return lax.ppermute(block, axis, route)


def silu_grad(value):
    sigmoid = jax.nn.sigmoid(value)
    return sigmoid * (1.0 + value * (1.0 - sigmoid))


def rotate_pairs(values, positions, direction):
    half_dim = values.shape[-1] // 2
    inverse = ROPE_BASE ** (-jnp.arange(half_dim).astype(jnp.float32) / half_dim)
    angles = positions[:, None] * inverse[None, :]
    cosine = jnp.cos(angles)[:, None, :]
    sine = direction * jnp.sin(angles)[:, None, :]
    first_half = values[..., :half_dim]
    second_half = values[..., half_dim:]
    return jnp.concatenate(
        [first_half * cosine - second_half * sine, second_half * cosine + first_half * sine],
        axis=-1,
    )


def dot_back(first_op, second_op):
    return lax.dot_general(
        first_op, second_op, (((1,), (1,)), ((), ())), preferred_element_type=jnp.float32
    )


def dot_rows(first_op, second_op):
    return lax.dot_general(
        first_op, second_op, (((0,), (0,)), ((), ())), preferred_element_type=jnp.float32
    )


def spread_to_all(block, axis):
    size = lax.axis_size(axis)
    copies = jnp.broadcast_to(block[None], (size,) + block.shape)
    return lax.all_to_all(copies, axis, split_axis=0, concat_axis=0, tiled=True)


def summed_parts(stacked, axis):
    got = lax.all_to_all(stacked, axis, split_axis=0, concat_axis=0, tiled=True)
    return jnp.sum(got.astype(jnp.float32), axis=0)


def ein(spec, first_op, second_op):
    return jnp.einsum(
        spec,
        first_op.astype(jnp.bfloat16),
        second_op.astype(jnp.bfloat16),
        preferred_element_type=jnp.float32,
    )


def on_device(
    x_in,
    in_weight,
    out_weight,
    gu_weight,
    down_weight,
    norm_gain,
    mixer_gain,
    ffn_gain,
    conv_weight,
    conv_bias,
    dt_bias,
    a_log,
    skip_gain,
    out_grad,
):
    f32 = jnp.float32
    half = jnp.bfloat16
    heads = lax.axis_size("head")
    ranges = lax.axis_size("ctx")
    ctx_place = lax.axis_index("ctx")
    head_place = lax.axis_index("head")
    tokens, width = x_in.shape
    rows = tokens * heads
    mix_heads = MH // heads
    attn_heads = AH // heads
    group_devices = heads // KVH
    dssm = MH * MP
    mine = mix_heads * MP
    local_cols = mine + 2 * NS
    qcols = attn_heads * HDIM
    rate_start = 2 * dssm + 2 * NS
    query_start = rate_start + MH
    key_start = query_start + AH * HDIM
    value_start = key_start + KVH * HDIM
    score_scale = 1.0 / math.sqrt(HDIM)
    count = rows // CHUNK
    w_rows = in_weight.shape[0]
    unit_rows = down_weight.shape[0]
    both = ("ctx", "head")

    def columns_for(target):
        kv = target // group_devices
        return jnp.concatenate(
            [
                in_weight[:, target * mine : (target + 1) * mine],
                in_weight[:, dssm + target * mine : dssm + (target + 1) * mine],
                in_weight[:, 2 * dssm : rate_start],
                in_weight[:, query_start + target * qcols : query_start + (target + 1) * qcols],
                in_weight[:, key_start + kv * HDIM : key_start + (kv + 1) * HDIM],
                in_weight[:, value_start + kv * HDIM : value_start + (kv + 1) * HDIM],
                in_weight[:, rate_start + target * mix_heads : rate_start + (target + 1) * mix_heads],
            ],
            axis=1,
        )

    in_parts = lax.all_to_all(
        jnp.stack([columns_for(target) for target in range(heads)]),
        "head",
        split_axis=0,
        concat_axis=0,
        tiled=True,
    ).reshape(heads * w_rows, -1)
    w_in = lax.all_gather(in_parts, "ctx", axis=0, tiled=True)
    x_all = spread_to_all(x_in, "head").reshape(rows, width)
    small = jnp.concatenate(
        [norm_gain, mixer_gain, ffn_gain, conv_weight.reshape(-1), conv_bias]
    )
    small_all = spread_to_all(small, both)
    cuts = [0]
    for piece in (norm_gain, mixer_gain, ffn_gain, conv_weight, conv_bias):
        cuts.append(cuts[-1] + piece.size)
    smalls = [small_all[:, cuts[i] : cuts[i + 1]].astype(f32) for i in range(5)]
    gain_one, gain_mix, gain_two = (smalls[i].reshape(-1) for i in range(3))
    conv_w = smalls[3].reshape(-1, KW)
    conv_b = smalls[4].reshape(-1)
    gu_split = gu_weight.reshape(w_rows, 2, ranges, heads, unit_rows)
    gu_parts = lax.all_to_all(
        gu_split.transpose(3, 0, 1, 2, 4).reshape(heads, w_rows, -1),
        "head",
        split_axis=0,
        concat_axis=0,
        tiled=True,
    ).reshape(heads * w_rows, -1)
    w_out = lax.all_gather(out_weight, both, axis=0, tiled=True)
    w_gu = lax.all_gather(gu_parts, "ctx", axis=0, tiled=True)
    w_down = lax.all_gather(down_weight, "ctx", axis=0, tiled=True)
    units = ranges * unit_rows

    inputs_all = x_all.astype(f32)
    rms_all = lax.rsqrt(jnp.mean(inputs_all * inputs_all, axis=1, keepdims=True) + EPSILON)
    normed = (inputs_all * rms_all * gain_one[None, :]).astype(half)
    proj = jnp.dot(normed, w_in, preferred_element_type=f32).astype(half)
    z_part = proj[:, :mine].astype(f32)
    xbc = proj[:, mine : mine + local_cols]
    at = mine + local_cols
    queries_raw = proj[:, at : at + qcols]
    keys_raw = proj[:, at + qcols : at + qcols + HDIM]
    values_raw = proj[:, at + qcols + HDIM : at + qcols + 2 * HDIM]
    rate_raw = proj[:, at + qcols + 2 * HDIM :]

    query_first = ctx_place * rows
    positions = (query_first + jnp.arange(rows)).astype(f32)
    q_rot = rotate_pairs(
        queries_raw.astype(f32).reshape(rows, attn_heads, HDIM), positions, 1.0
    ).astype(half)
    q_rows = q_rot.transpose(1, 0, 2).reshape(attn_heads * rows, HDIM)
    k_rot = (
        rotate_pairs(keys_raw.astype(f32).reshape(rows, 1, HDIM), positions, 1.0)
        .reshape(rows, HDIM)
        .astype(half)
    )
    kv_own = jnp.concatenate([k_rot, values_raw], axis=1)
    kv_all = spread_to_all(kv_own, "ctx")

    rim = passed_along(xbc[rows - (KW - 1) :], "ctx", 1)
    padded = jnp.concatenate([rim, xbc], axis=0).astype(f32)
    own_w = jnp.concatenate(
        [lax.dynamic_slice_in_dim(conv_w, head_place * mine, mine, 0), conv_w[dssm:]], axis=0
    )
    own_b = jnp.concatenate(
        [lax.dynamic_slice_in_dim(conv_b, head_place * mine, mine, 0), conv_b[dssm:]], axis=0
    )
    conv_pre = jnp.broadcast_to(own_b[None, :], (rows, local_cols))
    for offset in range(KW):
        conv_pre = conv_pre + padded[offset : offset + rows] * own_w[:, offset][None, :]
    conv_out = jax.nn.silu(conv_pre).astype(half)

    def by_chunk(value):
        return value.reshape(count, CHUNK, mix_heads, -1).transpose(0, 2, 1, 3)

    def from_chunk(value):
        return value.transpose(0, 2, 1, 3).reshape(rows, -1)

    mix_x = by_chunk(conv_out[:, :mine])
    bmat = conv_out[:, mine : mine + NS].reshape(count, CHUNK, NS)
    cmat = conv_out[:, mine + NS :].reshape(count, CHUNK, NS)
    dt_pre = (rate_raw.astype(f32) + dt_bias[None, :]).reshape(count, CHUNK, mix_heads)
    dt_pre = dt_pre.transpose(0, 2, 1)
    step = jax.nn.softplus(dt_pre)
    decay_rate = -jnp.exp(a_log)
    lower = jnp.arange(CHUNK)[:, None] >= jnp.arange(CHUNK)[None, :]
    tril = lower.astype(f32)
    cum = jnp.einsum(
        "nhs,ts->nht", step * decay_rate[None, :, None], tril, precision=PRECISE_MODE
    )
    within = jnp.exp(jnp.where(lower, cum[:, :, :, None] - cum[:, :, None, :], -jnp.inf))
    products = ein("ntm,nsm->nts", cmat, bmat)
    mixing = (products[:, None] * within * step[:, :, None, :]).astype(half)
    intra = ein("nhts,nhsp->nhtp", mixing, mix_x)
    x_f = mix_x.astype(f32)
    fade = jnp.exp(cum[:, :, -1:] - cum)
    reach = fade * step
    x_reach = (x_f * reach[..., None]).astype(half)
    ends = ein("nhsp,nsm->nhpm", x_reach, bmat)
    chunk_decay = jnp.exp(cum[:, :, -1])
    range_end = ends[0]
    range_decay = chunk_decay[0]
    for k in range(1, count):
        range_end = chunk_decay[k][:, None, None] * range_end + ends[k]
        range_decay = range_decay * chunk_decay[k]
    packed = jnp.concatenate(
        [range_end, jnp.broadcast_to(range_decay[:, None, None], (mix_heads, 8, NS))], axis=1
    )
    gathered = spread_to_all(packed, "ctx")
    decays = gathered[:, :, MP, 0]

    def weights(order, reached):
        factor = jnp.ones((mix_heads,), f32)
        found = [None] * ranges
        for j in order:
            found[j] = jnp.where(reached(j), factor, 0.0)
            factor = jnp.where(reached(j), factor * decays[j], factor)
        return jnp.stack(found)

    before = weights(range(ranges - 1, -1, -1), lambda j: j < ctx_place)
    after = weights(range(ranges), lambda j: j > ctx_place)
    states = [jnp.sum(before[:, :, None, None] * gathered[:, :, :MP], axis=0)]
    for k in range(count - 1):
        states.append(chunk_decay[k][:, None, None] * states[k] + ends[k])
    state = jnp.stack(states)
    grown = jnp.exp(cum)
    inter = ein("ntm,nhpm->nhtp", cmat, state) * grown[..., None]
    ssm_full = intra + inter + skip_gain[None, :, None, None] * x_f
    ssm_out = from_chunk(ssm_full.astype(half)).astype(f32)
    gated_mine = (ssm_out * jax.nn.silu(z_part)).astype(half)

    causal = jnp.arange(rows)[:, None] >= jnp.arange(rows)[None, :]
    causal = jnp.concatenate([causal] * attn_heads, axis=0)

    def key_block(number):
        piece = lax.dynamic_index_in_dim(kv_all, number, 0, False)
        return (piece[:, :HDIM], piece[:, HDIM:])

    scores = jnp.where(causal, dot_back(q_rows, k_rot) * score_scale, -jnp.inf)
    peak = jnp.max(scores, axis=1, keepdims=True)
    weight = jnp.exp(scores - peak)
    mass = jnp.sum(weight, axis=1, keepdims=True)
    total = jnp.dot(weight.astype(half), values_raw, preferred_element_type=f32)

    def attend(number, carry):
        peak, mass, total = carry
        keys_blk, vals_blk = key_block(number)
        scores = dot_back(q_rows, keys_blk) * score_scale
        new_peak = jnp.maximum(peak, jnp.max(scores, axis=1, keepdims=True))
        weight = jnp.exp(scores - new_peak)
        shrink = jnp.exp(peak - new_peak)
        mass = mass * shrink + jnp.sum(weight, axis=1, keepdims=True)
        total = total * shrink + jnp.dot(
            weight.astype(half), vals_blk, preferred_element_type=f32
        )
        return (new_peak, mass, total)

    peak, mass, total = lax.fori_loop(0, ctx_place, attend, (peak, mass, total))
    log_total = peak + jnp.log(mass)
    attn_rows = (total / mass).astype(half)
    attn_mine = attn_rows.reshape(attn_heads, rows, HDIM).transpose(1, 0, 2).reshape(rows, qcols)

    mixed_parts = lax.all_to_all(
        jnp.concatenate([gated_mine, attn_mine], axis=1).reshape(heads, tokens, -1),
        "head",
        split_axis=0,
        concat_axis=0,
        tiled=True,
    )
    gated = mixed_parts[:, :, :mine].transpose(1, 0, 2).reshape(tokens, dssm).astype(f32)
    attn_tok = mixed_parts[:, :, mine:].transpose(1, 0, 2).reshape(tokens, AH * HDIM)
    inputs = x_in.astype(f32)
    rms_in = lax.rsqrt(jnp.mean(inputs * inputs, axis=1, keepdims=True) + EPSILON)
    rms_mix = lax.rsqrt(jnp.mean(gated * gated, axis=1, keepdims=True) + EPSILON)
    mixed_norm = (gated * rms_mix * gain_mix[None, :]).astype(half)
    joined = jnp.concatenate([mixed_norm, attn_tok], axis=1)
    residual = inputs + jnp.dot(joined, w_out, preferred_element_type=f32)
    rms_ffn = lax.rsqrt(jnp.mean(residual * residual, axis=1, keepdims=True) + EPSILON)
    normed_ffn = (residual * rms_ffn * gain_two[None, :]).astype(half)
    normed_two = spread_to_all(normed_ffn, "head").reshape(rows, width)
    grad_all = spread_to_all(out_grad, "head").reshape(rows, width)
    gate_up = jnp.dot(normed_two, w_gu, preferred_element_type=f32)
    gate_part = gate_up[:, :units]
    up_part = gate_up[:, units:]
    activ = (jax.nn.silu(gate_part) * up_part).astype(half)
    d_activ = dot_back(grad_all, w_down)
    d_gate_up = jnp.concatenate(
        [d_activ * up_part * silu_grad(gate_part), d_activ * jax.nn.silu(gate_part)], axis=1
    ).astype(half)
    d_normed_ffn = summed_parts(
        dot_back(d_gate_up, w_gu).astype(half).reshape(heads, tokens, width), "head"
    )
    down_sum = lax.psum_scatter(
        dot_rows(activ, grad_all).astype(half), "ctx", scatter_dimension=0, tiled=True
    ).astype(f32)
    gu_sum = lax.psum_scatter(
        dot_rows(normed_two, d_gate_up).astype(half), "ctx", scatter_dimension=0, tiled=True
    )
    y_out = (
        residual
        + summed_parts(
            jnp.dot(activ, w_down, preferred_element_type=f32)
            .astype(half)
            .reshape(heads, tokens, width),
            "head",
        )
    ).astype(half)
    ffn_gain_grad = jnp.sum(d_normed_ffn * residual * rms_ffn, axis=0)
    scaled_ffn = gain_two[None, :] * d_normed_ffn
    d_residual = (
        out_grad.astype(f32)
        + rms_ffn * scaled_ffn
        - residual * rms_ffn**3 * jnp.mean(scaled_ffn * residual, axis=1, keepdims=True)
    )
    d_res_half = d_residual.astype(half)
    d_joined = dot_back(d_res_half, w_out)
    out_sum = lax.psum_scatter(
        dot_rows(joined, d_res_half).astype(half), both, scatter_dimension=0, tiled=True
    ).astype(f32)
    d_mixed = d_joined[:, :dssm]
    mixer_gain_grad = jnp.sum(d_mixed * gated * rms_mix, axis=0)
    scaled_mix = gain_mix[None, :] * d_mixed
    d_gated_tok = rms_mix * scaled_mix - gated * rms_mix**3 * jnp.mean(
        scaled_mix * gated, axis=1, keepdims=True
    )
    back_parts = jnp.concatenate(
        [
            d_gated_tok.astype(half).reshape(tokens, heads, mine),
            d_joined[:, dssm:].astype(half).reshape(tokens, heads, qcols),
        ],
        axis=2,
    ).transpose(1, 0, 2)
    back_got = lax.all_to_all(
        back_parts, "head", split_axis=0, concat_axis=0, tiled=True
    ).reshape(rows, mine + qcols)
    d_gated = back_got[:, :mine].astype(f32)
    d_z = d_gated * ssm_out * silu_grad(z_part)
    d_ssm = by_chunk((d_gated * jax.nn.silu(z_part)).astype(half))

    d_grown = (d_ssm.astype(f32) * grown[..., None]).astype(half)
    pulls = ein("nhtp,ntm->nhpm", d_grown, cmat)
    range_pull = pulls[count - 1]
    for k in range(count - 2, -1, -1):
        range_pull = chunk_decay[k][:, None, None] * range_pull + pulls[k]
    pulls_all = spread_to_all(range_pull.astype(half), "ctx").astype(f32)
    d_ends = [None] * count
    d_ends[count - 1] = jnp.sum(after[:, :, None, None] * pulls_all, axis=0)
    for k in range(count - 1, 0, -1):
        d_ends[k - 1] = chunk_decay[k][:, None, None] * d_ends[k] + pulls[k]
    d_end = jnp.stack(d_ends)

    d_rows = back_got[:, mine:].reshape(rows, attn_heads, HDIM).transpose(1, 0, 2)
    d_rows = d_rows.reshape(attn_heads * rows, HDIM)
    row_delta = jnp.sum(d_rows.astype(f32) * attn_rows.astype(f32), axis=1, keepdims=True)

    def back_block(scores, keys_blk, vals_blk):
        probs = jnp.exp(scores - log_total)
        d_probs = dot_back(d_rows, vals_blk)
        d_scores = (probs * (d_probs - row_delta)).astype(half)
        query_part = jnp.dot(d_scores, keys_blk, preferred_element_type=f32)
        key_part = dot_rows(d_scores, q_rows) * score_scale
        value_part = dot_rows(probs.astype(half), d_rows)
        return (query_part, jnp.concatenate([key_part, value_part], axis=1).astype(half))

    own_scores = jnp.where(causal, dot_back(q_rows, k_rot) * score_scale, -jnp.inf)
    query_grad, kv_own_grad = back_block(own_scores, k_rot, values_raw)

    def back_step(number, carry):
        query_grad, kv_grads = carry
        keys_blk, vals_blk = key_block(number)
        query_part, kv_part = back_block(
            dot_back(q_rows, keys_blk) * score_scale, keys_blk, vals_blk
        )
        kv_grads = lax.dynamic_update_index_in_dim(kv_grads, kv_part, number, 0)
        return (query_grad + query_part, kv_grads)

    kv_start = lax.dynamic_update_index_in_dim(
        jnp.zeros((ranges, rows, 2 * HDIM), half), kv_own_grad, ctx_place, 0
    )
    query_grad, kv_grads = lax.fori_loop(0, ctx_place, back_step, (query_grad, kv_start))
    kv_mine = summed_parts(kv_grads, "ctx")
    query_grad = (query_grad * score_scale).reshape(attn_heads, rows, HDIM).transpose(1, 0, 2)
    d_query = rotate_pairs(query_grad, positions, -1.0).reshape(rows, qcols)
    d_key = rotate_pairs(kv_mine[:, None, :HDIM], positions, -1.0).reshape(rows, HDIM)
    d_value = kv_mine[:, HDIM:]

    d_f = d_ssm.astype(f32)
    overlap = ein("nhtp,nhsp->nhts", d_ssm, mix_x) * within
    weighted = overlap * step[:, :, None, :]
    d_products = jnp.sum(weighted, axis=1)
    felt = overlap * products[:, None]
    felt_sum = jnp.sum(felt, axis=2)
    grad_step = felt_sum
    d_cum = jnp.sum(felt * step[:, :, None, :], axis=3) - step * felt_sum
    grad_b = ein("nts,ntm->nsm", d_products, cmat)
    grad_c = ein("nts,nsm->ntm", d_products, bmat)
    grad_x = ein("nhts,nhtp->nhsp", mixing, d_ssm)
    d_cum = d_cum + jnp.sum(d_f * inter, axis=3)
    grad_c = grad_c + ein("nhtp,nhpm->ntm", d_grown, state)
    d_reach_x = ein("nhpm,nsm->nhsp", d_end, bmat)
    grad_b = grad_b + ein("nhsp,nhpm->nsm", x_reach, d_end)
    grad_x = grad_x + reach[..., None] * d_reach_x + skip_gain[None, :, None, None] * d_f
    d_reach = jnp.sum(d_reach_x * x_f, axis=3)
    grad_step = grad_step + fade * d_reach
    moved = reach * d_reach
    last = jnp.sum(moved, axis=2) + chunk_decay * jnp.sum(d_end * state, axis=(2, 3))
    d_cum = d_cum - moved
    d_rate = jnp.einsum("nht,ts->nhs", d_cum, tril, precision=PRECISE_MODE) + last[:, :, None]
    grad_step = grad_step + d_rate * decay_rate[None, :, None]
    grad_decay = jnp.sum(d_rate * step, axis=(0, 2))
    skip_part = jnp.sum(d_f * x_f, axis=(0, 2, 3))
    d_dt_pre = grad_step * jax.nn.sigmoid(dt_pre)
    head_local = jnp.concatenate(
        [jnp.sum(d_dt_pre, axis=(0, 2)), grad_decay * decay_rate, skip_part]
    )
    d_rates = d_dt_pre.transpose(0, 2, 1).reshape(rows, mix_heads)

    d_conv_pre = jnp.concatenate(
        [from_chunk(grad_x), grad_b.reshape(rows, NS), grad_c.reshape(rows, NS)], axis=1
    ) * silu_grad(conv_pre)
    conv_b_local = jnp.sum(d_conv_pre, axis=0)
    conv_w_local = jnp.stack(
        [jnp.sum(d_conv_pre * padded[offset : offset + rows], axis=0) for offset in range(KW)],
        axis=1,
    )
    edge = passed_along(d_conv_pre[: KW - 1], "ctx", -1)
    d_long = jnp.concatenate([d_conv_pre, edge], axis=0)
    d_xbc = jnp.zeros((rows, local_cols), f32)
    for offset in range(KW):
        shift = KW - 1 - offset
        d_xbc = d_xbc + d_long[shift : shift + rows] * own_w[:, offset][None, :]
    d_proj = jnp.concatenate(
        [d_z, d_xbc, d_query, d_key, d_value, d_rates], axis=1
    ).astype(half)
    in_grad = dot_rows(normed, d_proj).astype(half)
    in_mine = summed_parts(in_grad.reshape(ranges, heads * w_rows, -1), "ctx").astype(half)
    d_normed = summed_parts(
        dot_back(d_proj, w_in).astype(half).reshape(heads, tokens, width), "head"
    )
    norm_gain_grad = jnp.sum(d_normed * inputs * rms_in, axis=0)
    scaled_in = gain_one[None, :] * d_normed
    x_grad = (
        d_residual
        + rms_in * scaled_in
        - inputs * rms_in**3 * jnp.mean(scaled_in * inputs, axis=1, keepdims=True)
    )

    gu_got = lax.all_to_all(
        gu_sum.reshape(heads, w_rows, -1), "head", split_axis=0, concat_axis=0, tiled=True
    ).astype(f32)
    gate_sum = (
        gu_got.reshape(heads, w_rows, 2, ranges, unit_rows)
        .transpose(1, 2, 3, 0, 4)
        .reshape(w_rows, -1)
    )
    in_got = lax.all_to_all(
        in_mine.reshape(heads, w_rows, -1), "head", split_axis=0, concat_axis=0, tiled=True
    ).astype(f32)

    def side_by_side(first, cols):
        return in_got[:, :, first : first + cols].transpose(1, 0, 2).reshape(w_rows, heads * cols)

    def grouped(first):
        piece = in_got[:, :, first : first + HDIM].reshape(KVH, group_devices, w_rows, HDIM)
        return jnp.sum(piece, axis=1).transpose(1, 0, 2).reshape(w_rows, KVH * HDIM)

    input_sum = jnp.concatenate(
        [
            side_by_side(0, mine),
            side_by_side(mine, mine),
            jnp.sum(in_got[:, :, 2 * mine : at], axis=0),
            side_by_side(at + qcols + 2 * HDIM, mix_heads),
            side_by_side(at, qcols),
            grouped(at + qcols),
            grouped(at + qcols + HDIM),
        ],
        axis=1,
    )

    def placed_rows(local):
        full = jnp.zeros((dssm + 2 * NS,) + local.shape[1:], f32)
        full = lax.dynamic_update_slice_in_dim(full, local[:mine], head_place * mine, 0)
        return lax.dynamic_update_slice_in_dim(full, local[mine:], dssm, 0)

    devices = ranges * heads
    own_head = (jnp.arange(devices) % heads == head_place).astype(f32)
    small_grads = jnp.concatenate(
        [
            norm_gain_grad.reshape(devices, -1),
            mixer_gain_grad.reshape(devices, -1),
            ffn_gain_grad.reshape(devices, -1),
            placed_rows(conv_w_local).reshape(devices, -1),
            placed_rows(conv_b_local).reshape(devices, -1),
            own_head[:, None] * head_local[None, :],
        ],
        axis=1,
    )
    small_sum = jnp.sum(
        lax.all_to_all(small_grads, both, split_axis=0, concat_axis=0, tiled=True), axis=0
    )
    head_sums = small_sum[cuts[5] :].reshape(3, mix_heads)
    return (
        y_out,
        x_grad,
        input_sum,
        out_sum,
        gate_sum,
        down_sum,
        small_sum[cuts[0] : cuts[1]],
        small_sum[cuts[1] : cuts[2]],
        small_sum[cuts[2] : cuts[3]],
        small_sum[cuts[3] : cuts[4]].reshape(-1, KW),
        small_sum[cuts[4] : cuts[5]],
        head_sums[0],
        head_sums[1],
        head_sums[2],
    )


def solution(mesh):
    placed = (
        P(("ctx", "head"), None),
        P(("ctx", "head"), None),
        P(("ctx", "head"), None),
        P(("ctx", "head"), None),
        P(("ctx", "head"), None),
        P(("ctx", "head")),
        P(("ctx", "head")),
        P(("ctx", "head")),
        P(("ctx", "head"), None),
        P(("ctx", "head")),
        P("head"),
        P("head"),
        P("head"),
        P(("ctx", "head"), None),
    )
    return jax.shard_map(
        on_device,
        mesh=mesh,
        in_specs=placed,
        out_specs=(
            P(("ctx", "head"), None),
            P(("ctx", "head"), None),
            P(("ctx", "head"), None),
            P(("ctx", "head"), None),
            P(("ctx", "head"), None),
            P(("ctx", "head"), None),
            P(("ctx", "head")),
            P(("ctx", "head")),
            P(("ctx", "head")),
            P(("ctx", "head"), None),
            P(("ctx", "head")),
            P("head"),
            P("head"),
            P("head"),
        ),
        check_vma=False,
    )
```
